32 devices in a mesh: groups: 2 (over y), wide: 8 (over z, x), narrow: 2 (over core).
Axes of the slice: x: 2, y: 2, z: 4, core: 2. Of those that a mesh axis runs over, the one named last changes fastest.
Arguments:
- candidates: bfloat16 [16, 2048, 512], P('groups', ('wide', 'narrow')), parts along dimension 0, may hold values from -6 to 6
- pre_inner: bfloat16 [512, 512], replicated, may hold values from -0.25 to 0.25
- pre_bias: float32 [512], replicated, may hold values from -3 to 3
- pre_outer: bfloat16 [512, 512], replicated, may hold values from -0.25 to 0.25
- user_vector: bfloat16 [16, 512], P('groups'), parts along dimension 0, may hold values from -0.25 to 0.25
- kept_index: int32 [16, 512], P('groups'), parts along dimension 0, may hold values from 0 to 2047, as said below
- slot_request: int32 [16], P('groups'), parts along dimension 0, may hold values from 0 to 7, each once
- history_kv: bfloat16 [16, 2, 512, 512], P(('groups', 'wide'), None, None, 'narrow'), parts along dimension 0, may hold values from -6 to 6
- history_bias: float32 [16, 8, 512], P(('groups', 'wide'), 'narrow'), parts along dimension 0, may hold values from -8 to 404
- history_length: int32 [16], P(('groups', 'wide')), parts along dimension 0, may hold values from 64 to 512, as said below
- query_weight: bfloat16 [512, 512], replicated, may hold values from -0.25 to 0.25
- norm_gain: float32 [512], replicated, may hold values from 0.1 to 1.9
- expert_weight: bfloat16 [8, 512, 256], P('narrow'), may hold values from -0.25 to 0.25
- gate_weight: bfloat16 [512, 64], replicated, may hold values from -0.25 to 0.25
- gate_bias: float32 [8, 8], replicated, may hold values from -4 to 401
- tower_inner: bfloat16 [8, 256, 128], P('narrow'), may hold values from -0.375 to 0.375
- tower_outer: bfloat16 [8, 128], P('narrow'), may hold values from -0.5 to 0.5
Outputs:
- prerank_score: float32 [16, 2048], P('groups', ('wide', 'narrow')), parts along dimension 0
- rank_score: float32 [8, 16, 2048], P(None, 'groups', ('wide', 'narrow')), parts along dimension 1
The draws below stay inside these ranges and needn't reach their ends.
There are 2 independent parts, one for each index of `groups`. The reference program is written for one: setup_inputs(seed, part) draws one part's arguments, and reference() takes and returns one part's arrays. A program takes and returns all parts, laid end to end along the dimension named above; an argument that names none is the same for every part. Nothing has to cross between parts.
Inputs may be any that keep to these rules, and one draw needn't show every extreme that they name: `kept_index`: each row holds 512 distinct candidate numbers; of the candidates of one request in one aligned block of 128 numbers at most 64 are kept, and exactly 64 in some block of every request. `slot_request`: a permutation; slot s belongs to ranking group s. `history_length`: at least one entry equals 512.
All inputs are finite; a program needn't handle non-finite values.
Results may differ from the reference program's by a relative error of at most 0.0085.
Values may be sent and summed in bfloat16 or wider, within the bound.
A program may use at most 64 MiB of HBM per device.

```python
import jax
import jax.numpy as jnp
from jax import lax

F = 512
PH = 512
D = 512
H = 8
DH = 64
EXPERTS = 8
TASKS = 8
EH = 256
TH = 128
KEEP = 512
C = 2048
L = 512
R = 8
N_WIDE = 8
N_NARROW = 2


def draw_kept_index(key, part):
    shards = N_WIDE * N_NARROW
    shard_len = C // shards
    mean_kept = KEEP // shards
    order_key = jax.random.fold_in(key, 11)
    pair_key = jax.random.fold_in(key, 12)
    inner_key = jax.random.fold_in(key, 13)
    list_key = jax.random.fold_in(key, 14)
    order_score = jax.random.randint(order_key, (R, shards), 0, 1 << 20) * shards + jnp.arange(shards, dtype=jnp.int32)[None, :]
    shard_order = jnp.argsort(order_score, axis=1, stable=True)
    placed = jnp.argsort(shard_order, axis=1, stable=True)
    shifts = jax.random.randint(pair_key, (R, shards // 2), -mean_kept, mean_kept + 1)
    shifts = jnp.where(jnp.arange(shards // 2)[None, :] == 0, mean_kept, shifts)
    paired = jnp.concatenate([mean_kept + shifts, mean_kept - shifts], axis=1)
    counts = jnp.take_along_axis(paired, placed, axis=1)
    inner_score = jax.random.randint(inner_key, (R, shards, shard_len), 0, 1 << 20) * shard_len + jnp.arange(shard_len, dtype=jnp.int32)[None, None, :]
    inner_rank = jnp.argsort(jnp.argsort(inner_score, axis=2, stable=True), axis=2, stable=True)
    chosen = (inner_rank < counts[:, :, None]).reshape(R, C)
    ordered = jnp.argsort(jnp.where(chosen, 0, 1), axis=1, stable=True)[:, :KEEP]
    list_score = jax.random.randint(list_key, (R, KEEP), 0, 1 << 20) * KEEP + jnp.arange(KEEP, dtype=jnp.int32)[None, :]
    shuffle = jnp.argsort(list_score, axis=1, stable=True)
    return jnp.take_along_axis(ordered, shuffle, axis=1).astype(jnp.int32)


def draw_history_length(key, part):
    lengths = jax.random.randint(jax.random.fold_in(key, 21), (R,), L // 8, L + 1)
    longest = jax.random.randint(jax.random.fold_in(key, 22), (), 0, R)
    return jnp.where(jnp.arange(R) == longest, L, lengths).astype(jnp.int32)


def draw_history_bias(key, part):
    noise_key = jax.random.fold_in(key, 31)
    return jnp.clip(2.0 * jax.random.normal(noise_key, (R, H, L), jnp.float32), -8.0, 8.0)


def draw_gate_bias(key, part):
    noise_key = jax.random.fold_in(key, 41)
    return jnp.clip(jax.random.normal(noise_key, (TASKS, EXPERTS), jnp.float32), -4.0, 4.0)


def shard_levels(key, extent, pieces, low, high):
    loudness, own = 1.0, jax.random.fold_in(key, 6)
    for axis_at, parts in pieces:
        draws = jnp.exp(jax.random.uniform(jax.random.fold_in(own, axis_at), (parts,), jnp.float32, low / len(pieces), high / len(pieces)))
        loudness = loudness * jnp.repeat(draws, extent[axis_at] // parts).reshape([-1 if axis == axis_at else 1 for axis in range(len(extent))])
    return loudness


def centred(rng, extent, width, most, cuts=(), kind=jnp.bfloat16):
    values = jax.random.normal(rng, extent, jnp.float32) * width
    if len(cuts) > 0:
        values = shard_levels(rng, extent, cuts, -0.22, 0.18) * values
    return jnp.clip(values, min=-most, max=most).astype(kind)


def setup_inputs(seed: int = 0, part: int = 0) -> dict:
    splits = jax.random.split(jax.random.key(seed), 18)
    part_keys = jax.random.split(jax.random.fold_in(splits[17], part), 18)
    candidates = centred(part_keys[0], (R, C, F), 1.0, 6.0, ((1, 16),))
    pre_inner = centred(splits[1], (F, PH), F ** -0.5, 0.25)
    pre_bias = centred(splits[2], (PH,), 0.5, 3.0, (), jnp.float32)
    pre_outer = centred(splits[3], (PH, D), PH ** -0.5, 0.25)
    user_vector = centred(part_keys[4], (R, D), D ** -0.5, 0.25)
    kept_index = draw_kept_index(jax.random.fold_in(jax.random.fold_in(splits[17], part), 71), part)
    slot_request = jax.random.permutation(part_keys[6], R).astype(jnp.int32)
    history_kv = centred(part_keys[7], (R, 2, L, H * DH), 1.0, 6.0, ((0, 8), (3, 2)))
    history_bias = draw_history_bias(jax.random.fold_in(jax.random.fold_in(splits[17], part), 71), part)
    history_length = draw_history_length(jax.random.fold_in(jax.random.fold_in(splits[17], part), 71), part)
    query_weight = centred(splits[10], (D, H * DH), D ** -0.5, 0.25)
    norm_gain = jnp.clip(1.0 + 0.18 * jax.random.normal(splits[11], (D,), jnp.float32), 0.1, 1.9)
    expert_weight = centred(splits[12], (EXPERTS, D, EH), D ** -0.5, 0.25, ((0, 2),))
    gate_weight = centred(splits[13], (D, TASKS * EXPERTS), D ** -0.5, 0.25)
    gate_bias = draw_gate_bias(jax.random.fold_in(splits[17], 71), part)
    tower_inner = centred(splits[15], (TASKS, EH, TH), EH ** -0.5, 0.375, ((0, 2),))
    tower_outer = centred(splits[16], (TASKS, TH), TH ** -0.5, 0.5, ((0, 2),))
    return dict(candidates=candidates, pre_inner=pre_inner, pre_bias=pre_bias, pre_outer=pre_outer, user_vector=user_vector, kept_index=kept_index, slot_request=slot_request, history_kv=history_kv, history_bias=history_bias, history_length=history_length, query_weight=query_weight, norm_gain=norm_gain, expert_weight=expert_weight, gate_weight=gate_weight, gate_bias=gate_bias, tower_inner=tower_inner, tower_outer=tower_outer)


def reference(candidates, pre_inner, pre_bias, pre_outer, user_vector, kept_index, slot_request, history_kv, history_bias, history_length, query_weight, norm_gain, expert_weight, gate_weight, gate_bias, tower_inner, tower_outer):
    score_scale = float(DH) ** (-0.5)

    def per_slot(slot_index):
        request = slot_request[slot_index]
        features = candidates[request]
        hidden_pre = jax.nn.relu(jnp.dot(features, pre_inner, preferred_element_type=jnp.float32) + pre_bias).astype(jnp.bfloat16)
        embedded = jnp.dot(hidden_pre, pre_outer, preferred_element_type=jnp.float32).astype(jnp.bfloat16)
        pre_row = jnp.dot(embedded, user_vector[request], preferred_element_type=jnp.float32)
        kept_ids = kept_index[request].astype(jnp.int32)
        kept_rows = embedded[kept_ids]
        queries = jnp.dot(kept_rows, query_weight, preferred_element_type=jnp.float32).astype(jnp.bfloat16).reshape(KEEP, H, DH)
        history_keys = history_kv[slot_index, 0].reshape(L, H, DH)
        history_values = history_kv[slot_index, 1].reshape(L, H, DH)
        scores = jnp.einsum('khd,lhd->hkl', queries.astype(jnp.float32), history_keys.astype(jnp.float32)) * score_scale
        scores = scores + history_bias[slot_index][:, None, :]
        visible = jnp.arange(L, dtype=jnp.int32) < history_length[slot_index]
        scores = jnp.where(visible[None, None, :], scores, -jnp.inf)
        row_max = lax.optimization_barrier(jnp.max(scores, axis=2, keepdims=True))
        powers = jnp.exp(scores - row_max)
        weights = (powers / lax.optimization_barrier(jnp.sum(powers, axis=2, keepdims=True))).astype(jnp.bfloat16)
        attended = jnp.einsum('hkl,lhd->khd', weights.astype(jnp.float32), history_values.astype(jnp.float32)).astype(jnp.bfloat16).reshape(KEEP, H * DH)
        mixed_in = kept_rows.astype(jnp.float32) + attended.astype(jnp.float32)
        normed = (mixed_in * lax.rsqrt(lax.optimization_barrier(jnp.mean(mixed_in * mixed_in, axis=1, keepdims=True)) + 1e-06) * norm_gain).astype(jnp.bfloat16)
        expert_out = jax.nn.relu(jnp.einsum('kd,edh->keh', normed.astype(jnp.float32), expert_weight.astype(jnp.float32))).astype(jnp.bfloat16)
        logits = jnp.dot(normed, gate_weight, preferred_element_type=jnp.float32).reshape(KEEP, TASKS, EXPERTS) + gate_bias[None]
        logit_max = lax.optimization_barrier(jnp.max(logits, axis=2, keepdims=True))
        gate_pow = jnp.exp(logits - logit_max)
        gate_probs = (gate_pow / lax.optimization_barrier(jnp.sum(gate_pow, axis=2, keepdims=True))).astype(jnp.bfloat16)
        mixture = jnp.einsum('kte,keh->kth', gate_probs.astype(jnp.float32), expert_out.astype(jnp.float32)).astype(jnp.bfloat16)
        tower_act = jax.nn.relu(jnp.einsum('kth,thj->ktj', mixture.astype(jnp.float32), tower_inner.astype(jnp.float32))).astype(jnp.bfloat16)
        task_logit = jnp.einsum('ktj,tj->kt', tower_act.astype(jnp.float32), tower_outer.astype(jnp.float32))
        rank_row = jnp.zeros((TASKS, C), jnp.float32).at[:, kept_ids].set(task_logit.T)
        return (pre_row, rank_row)
    pre_rows, rank_rows = lax.map(per_slot, jnp.arange(R, dtype=jnp.int32))
    order_ids = slot_request.astype(jnp.int32)
    prerank_score = jnp.zeros((R, C), jnp.float32).at[order_ids].set(pre_rows)
    rank_full = jnp.zeros((R, TASKS, C), jnp.float32).at[order_ids].set(rank_rows)
    return (prerank_score, jnp.transpose(rank_full, (1, 0, 2)))
```

```python
import functools

import jax
import jax.numpy as jnp
from jax import lax
from jax.experimental import pallas as pl
from jax.experimental.pallas import tpu as pltpu
from jax.sharding import PartitionSpec as P

F32 = jnp.float32
BF16 = jnp.bfloat16
MESH = pl.DeviceIdType.MESH


def quotient(x, n):
    if n & (n - 1) == 0:
        return lax.shift_right_logical(x, jnp.full_like(x, n.bit_length() - 1))
    return lax.div(x, jnp.full_like(x, n))


def iota(shape, dim):
    return lax.broadcasted_iota(jnp.int32, shape, dim)


def loop(count, body):
    if count <= 16:
        for i in range(count):
            body(i)
    else:
        lax.fori_loop(0, count, lambda i, _: (body(i), 0)[1], 0)


def dot(a, b, dims=((1,), (0,))):
    return lax.dot_general(a, b, (dims, ((), ())), preferred_element_type=F32)


def cascade(
    wide,
    narrow,
    block,
    slot_request,
    slot_of,
    length,
    kept,
    user,
    pre_bias,
    norm_gain,
    gate_bias,
    cand_hbm,
    inner_hbm,
    outer_hbm,
    query_hbm,
    kv_hbm,
    bias_hbm,
    expert_hbm,
    gate_hbm,
    tower_hbm,
    last_hbm,
    score_out,
    rank_out,
    cand,
    inner,
    outer,
    query,
    kv,
    bias,
    expert,
    gate,
    tower,
    last,
    outgoing,
    arrived,
    compaction,
    expert_out,
    mixed,
    going,
    returned,
    local_sem,
    row_send,
    row_recv,
    swap_send,
    swap_recv,
    back_send,
    back_recv,
):
    w = lax.axis_index("wide")
    n = lax.axis_index("narrow")
    shards = wide * narrow
    me = w * narrow + n
    requests, shard_len, _ = cand.shape
    kept_count = kept.shape[1]
    rows = kept_count // narrow
    tasks = gate_bias.shape[0]
    experts = gate_bias.shape[1]
    heads_here = bias.shape[1]

    barrier = pltpu.get_barrier_semaphore()

    def greet(k):
        d = lax.rem(me + k + 1, shards)
        pl.semaphore_signal(
            barrier,
            inc=1,
            device_id={"wide": d // narrow, "narrow": lax.rem(d, narrow)},
            device_id_type=MESH,
        )

    loop(shards - 1, greet)

    plain = [
        pltpu.make_async_copy(src, dst, local_sem.at[k])
        for k, (src, dst) in enumerate(
            (
                (cand_hbm, cand),
                (inner_hbm, inner),
                (outer_hbm, outer),
                (query_hbm, query),
                (gate_hbm, gate),
            )
        )
    ]
    shared = ((kv_hbm.at[0], kv), (bias_hbm.at[0], bias), (expert_hbm, expert), (tower_hbm, tower), (last_hbm, last))
    own = [
        pltpu.make_async_copy(src, dst.at[n], local_sem.at[len(plain) + k])
        for k, (src, dst) in enumerate(shared)
    ]
    for copy in plain + own:
        copy.start()

    base = me * shard_len
    local = base + iota((shard_len, 1), 0)

    def pack(req, emb):
        row = kept[pl.ds(req, 1), :]
        below = jnp.sum((row < local).astype(F32), axis=1, keepdims=True).astype(jnp.int32)
        here = jnp.sum((row == local).astype(F32), axis=1, keepdims=True) > 0.5
        start = below[0:1]
        level = quotient(below, narrow)
        core = below - level * narrow
        place = level - quotient(start + (narrow - 1) - core, narrow)
        place = jnp.where(here, core * block + place, -1)
        packing = (place == iota((1, narrow * block), 1)).astype(F32).astype(BF16)
        return dot(packing, emb, ((0,), (0,))).astype(BF16)

    def score(req, emb):
        every = dot(user[...], emb, ((1,), (1,)))
        score_out[...] += jnp.where(iota((requests, 1), 0) == req, every, 0.0)

    score_out[...] = jnp.zeros_like(score_out)
    for copy in plain[:3]:
        copy.wait()

    def row_copy(i, g, p):
        return pltpu.make_async_remote_copy(
            src_ref=outgoing.at[i, p],
            dst_ref=arrived.at[me],
            send_sem=row_send.at[i, p],
            recv_sem=row_recv.at[me],
            device_id={"wide": g, "narrow": p},
            device_id_type=MESH,
        )

    def embed(x):
        hidden = jnp.maximum(dot(x, inner[...]) + pre_bias[...], 0.0).astype(BF16)
        return dot(hidden, outer[...]).astype(BF16)

    def serve(i, g, req, emb):
        packed = pack(req, emb)
        for p in range(narrow):
            outgoing[i, p] = packed[p * block : (p + 1) * block]

    def send(i, g):
        for p in range(narrow):
            row_copy(i, g, p).start()

    def swaps(k):
        other = lax.rem(n + k, narrow)
        return [
            pltpu.make_async_remote_copy(
                src_ref=src,
                dst_ref=dst.at[n],
                send_sem=swap_send.at[k, a],
                recv_sem=swap_recv.at[k, a],
                device_id={"narrow": other},
                device_id_type=MESH,
            )
            for a, (src, dst) in enumerate(shared)
        ]

    pair = 2 if shard_len % 16 == 0 and wide % 2 == 0 and wide <= 16 else 1
    if pair == 2:
        order = sorted(range(wide), key=lambda d: (abs(2 * d - wide), d))
        order = [d for d in order if d] + [0]
        for first in range(0, wide, 2):
            slots = [lax.rem(w + order[first + a], wide) for a in range(2)]
            reqs = [slot_request[g] for g in slots]
            both = embed(jnp.concatenate([cand[r] for r in reqs], axis=0))
            for a in range(2):
                emb = both[a * shard_len : (a + 1) * shard_len]
                serve(first + a, slots[a], reqs[a], emb)
                score(reqs[a], emb)
            if first == 0:
                pl.semaphore_wait(barrier, shards - 1)
            for a in range(2):
                if order[first + a]:
                    send(first + a, slots[a])
            if first == 2 or wide == 2:
                for k in range(1, narrow):
                    for copy in swaps(k):
                        copy.start()
    else:
        pl.semaphore_wait(barrier, shards - 1)
        for k in range(1, narrow):
            for copy in swaps(k):
                copy.start()

        def one(i):
            g = lax.rem(w + i + 1, wide)
            req = slot_request[g]
            emb = embed(cand[req])
            serve(i, g, req, emb)
            score(req, emb)

        def one_sent(i):
            one(i)
            send(i, lax.rem(w + i + 1, wide))

        loop(wide - 1, one_sent)
        one(wide - 1)
    for k in range(1, narrow):
        row_copy(wide - 1, w, lax.rem(n + k, narrow)).start()
    arrived[me] = outgoing[wide - 1, n]

    request = slot_request[w]
    row = kept[pl.ds(request, 1), :].astype(F32)
    column = jnp.transpose(jnp.broadcast_to(row, (128, kept_count)))[:, 0:1]
    rank = jnp.sum((column < row).astype(F32), axis=0, keepdims=True)
    line = iota((rows, 1), 0)
    wanted = (line * narrow + n).astype(F32)
    chosen = jnp.sum(jnp.where(rank == wanted, row, 0.0), axis=1, keepdims=True)
    chosen = chosen.astype(jnp.int32)
    shard = quotient(chosen, shard_len)
    start = jnp.sum(
        (row < (shard * shard_len).astype(F32)).astype(F32), axis=1, keepdims=True
    ).astype(jnp.int32)
    spot = shard * block + line - quotient(start + (narrow - 1) - n, narrow)
    compaction[...] = (spot == iota((1, shards * block), 1)).astype(F32).astype(BF16)

    for copy in plain[3:] + own:
        copy.wait()
    for k in range(1, narrow):
        for copy in swaps(k):
            copy.wait_recv()

    def rows_in(k):
        d = lax.rem(me + k + 1, shards)
        pltpu.make_async_remote_copy(
            src_ref=outgoing.at[0, 0],
            dst_ref=arrived.at[d],
            send_sem=row_send.at[0, 0],
            recv_sem=row_recv.at[d],
            device_id={"wide": d // narrow, "narrow": lax.rem(d, narrow)},
            device_id_type=MESH,
        ).wait_recv()

    loop(shards - 1, rows_in)
    width = arrived.shape[2]
    embedded = dot(compaction[...], arrived[...].reshape(shards * block, width)).astype(BF16)
    heads = heads_here * narrow
    size = query.shape[1] // heads
    queries = dot(embedded, query[...]).astype(BF16).astype(F32) * float(size) ** (-0.5)
    span = kv.shape[2]
    seen = iota((1, span), 1) < length[0]
    side = 128 // size if 128 % size == 0 and heads_here % (128 // size) == 0 else 1
    strip = side * size
    lane = iota((1, strip), 1)
    pieces = []
    for first in range(0, heads, side):
        c, h = first // heads_here, first % heads_here
        keys = kv[c, 0, :, h * size : h * size + strip]
        values = kv[c, 1, :, h * size : h * size + strip]
        q = queries[:, first * size : first * size + strip]
        out = None
        for a in range(side):
            mine = (lane >= a * size) & (lane < (a + 1) * size)
            s = dot(jnp.where(mine, q, 0.0).astype(BF16), keys, ((1,), (1,)))
            s = s + jnp.where(seen, bias[c, h + a : h + a + 1, :], -jnp.inf)
            top = jnp.max(s, axis=1, keepdims=True)
            powers = jnp.exp(s - top)
            total = jnp.sum(powers, axis=1, keepdims=True)
            part = dot(powers.astype(BF16), values) / total
            out = part if out is None else jnp.where(mine, part, out)
        pieces.append(out.astype(BF16))
    attended = jnp.concatenate(pieces, axis=1)
    u = embedded.astype(F32) + attended.astype(F32)
    normed = (
        u * lax.rsqrt(jnp.mean(u * u, axis=1, keepdims=True) + 1e-06) * norm_gain[...]
    ).astype(BF16)

    logits = dot(gate[...], normed, ((0,), (1,)))
    diagonal = iota((experts, experts), 0) == iota((experts, experts), 1)
    probs = []
    for t in range(tasks):
        offset = jnp.sum(
            jnp.where(diagonal, gate_bias[t : t + 1, :], 0.0), axis=1, keepdims=True
        )
        x = logits[t * experts : (t + 1) * experts] + offset
        x = jnp.exp(x - jnp.max(x, axis=0, keepdims=True))
        probs.append(x / jnp.sum(x, axis=0, keepdims=True))
    fill = -(tasks * experts) % 128
    if fill:
        probs.append(jnp.zeros((fill, rows), F32))
    probs = jnp.transpose(jnp.concatenate(probs, axis=0).astype(BF16).astype(F32))

    experts_here = expert.shape[1]
    for e in range(experts):
        out = dot(normed, expert[e // experts_here, e % experts_here])
        expert_out[e] = jnp.maximum(out, 0.0).astype(BF16).astype(F32)
    step = 64 if rows % 64 == 0 else rows
    for t in range(tasks):
        for r in range(0, rows, step):
            acc = None
            for e in range(experts):
                k = t * experts + e
                term = probs[r : r + step, k : k + 1] * expert_out[e, r : r + step]
                acc = term if acc is None else acc + term
            mixed[t, r : r + step] = acc.astype(BF16)
    tasks_here = tower.shape[1]
    final = jnp.zeros((tasks, rows), F32)
    for t in range(tasks):
        c, h = t // tasks_here, t % tasks_here
        act = jnp.maximum(dot(mixed[t], tower[c, h]), 0.0).astype(BF16)
        weights = last[c, h : h + 1, :].astype(F32)
        weights = jnp.where(iota((tasks, 1), 0) == t, weights, 0.0).astype(BF16)
        final = final + dot(weights, act, ((1,), (1,)))

    high = final.astype(BF16)
    rest = final - high.astype(F32)
    middle = rest.astype(BF16)
    low = (rest - middle.astype(F32)).astype(BF16)
    lanes = going.shape[2]

    def back_copy(d):
        return pltpu.make_async_remote_copy(
            src_ref=going.at[d],
            dst_ref=returned.at[me],
            send_sem=back_send.at[d],
            recv_sem=back_recv.at[me],
            device_id={"wide": d // narrow, "narrow": lax.rem(d, narrow)},
            device_id_type=MESH,
        )

    def scatter(k):
        d = lax.rem(me + k + 1, shards)
        spread = (chosen == d * shard_len + iota((1, lanes), 1)).astype(F32).astype(BF16)
        going[d] = dot(high, spread) + dot(middle, spread) + dot(low, spread)

    def scatter_send(k):
        scatter(k)
        back_copy(lax.rem(me + k + 1, shards)).start()

    loop(shards - 1, scatter_send)
    scatter(shards - 1)
    returned[me] = going[me]

    def back_in(k):
        d = lax.rem(me + k + 1, shards)
        pltpu.make_async_remote_copy(
            src_ref=going.at[0],
            dst_ref=returned.at[d],
            send_sem=back_send.at[0],
            recv_sem=back_recv.at[d],
            device_id={"wide": d // narrow, "narrow": lax.rem(d, narrow)},
            device_id_type=MESH,
        ).wait_recv()

    loop(shards - 1, back_in)

    def deliver(r):
        total = returned[slot_of[r] * narrow]
        for p in range(1, narrow):
            total = total + returned[slot_of[r] * narrow + p]
        rank_out[r] = total[:, :shard_len]

    loop(requests, deliver)

    def rows_out(i):
        for p in range(narrow):
            row_copy(i, w, p).wait_send()

    loop(wide - 1, rows_out)
    for k in range(1, narrow):
        row_copy(wide - 1, w, lax.rem(n + k, narrow)).wait_send()
        for copy in swaps(k):
            copy.wait_send()
    loop(shards - 1, lambda k: back_copy(lax.rem(me + k + 1, shards)).wait_send())


def on_device(
    candidates,
    pre_inner,
    pre_bias,
    pre_outer,
    user_vector,
    kept_index,
    slot_request,
    history_kv,
    history_bias,
    history_length,
    query_weight,
    norm_gain,
    expert_weight,
    gate_weight,
    gate_bias,
    tower_inner,
    tower_outer,
):
    wide = lax.axis_size("wide")
    narrow = lax.axis_size("narrow")
    shards = wide * narrow
    requests, shard_len, features = candidates.shape
    kept_count = kept_index.shape[1]
    assert history_kv.shape[0] == 1 and requests == wide and kept_count % narrow == 0
    capacity = 2 * kept_count // shards
    block = -(-capacity // narrow)
    block = -(-block // 16) * 16
    rows = kept_count // narrow
    width = pre_outer.shape[1]
    tasks, experts = gate_bias.shape
    hidden = expert_weight.shape[2]
    lanes = max(shard_len, 128)
    ids = jnp.arange(requests, dtype=jnp.int32)
    slot_of = jnp.sum(jnp.where(slot_request[None, :] == ids[:, None], ids[None, :], 0), axis=1)
    smem = pl.BlockSpec(memory_space=pltpu.SMEM)
    vmem = pl.BlockSpec(memory_space=pltpu.VMEM)
    hbm = pl.BlockSpec(memory_space=pl.ANY)

    def whole(x):
        return pltpu.VMEM(x.shape, x.dtype)

    def both(x):
        return pltpu.VMEM((narrow, *x.shape), x.dtype)

    score, rank = pl.pallas_call(
        functools.partial(cascade, wide, narrow, block),
        out_shape=(
            jax.ShapeDtypeStruct((requests, shard_len), F32),
            jax.ShapeDtypeStruct((requests, tasks, shard_len), F32),
        ),
        in_specs=[smem] * 3 + [vmem] * 5 + [hbm] * 10,
        out_specs=(vmem, vmem),
        scratch_shapes=[
            whole(candidates),
            whole(pre_inner),
            whole(pre_outer),
            whole(query_weight),
            pltpu.VMEM((narrow, *history_kv.shape[1:]), BF16),
            pltpu.VMEM((narrow, *history_bias.shape[1:]), F32),
            both(expert_weight),
            whole(gate_weight),
            both(tower_inner),
            both(tower_outer),
            pltpu.VMEM((wide, narrow, block, width), BF16),
            pltpu.VMEM((shards, block, width), BF16),
            pltpu.VMEM((rows, shards * block), BF16),
            pltpu.VMEM((experts, rows, hidden), F32),
            pltpu.VMEM((tasks, rows, hidden), BF16),
            pltpu.VMEM((shards, tasks, lanes), F32),
            pltpu.VMEM((shards, tasks, lanes), F32),
            pltpu.SemaphoreType.DMA((10,)),
            pltpu.SemaphoreType.DMA((wide, narrow)),
            pltpu.SemaphoreType.DMA((shards,)),
            pltpu.SemaphoreType.DMA((narrow, 5)),
            pltpu.SemaphoreType.DMA((narrow, 5)),
            pltpu.SemaphoreType.DMA((shards,)),
            pltpu.SemaphoreType.DMA((shards,)),
        ],
        compiler_params=pltpu.CompilerParams(
            collective_id=0, has_side_effects=True, vmem_limit_bytes=56 * 1024 * 1024
        ),
    )(
        slot_request,
        slot_of,
        history_length,
        kept_index,
        user_vector,
        pre_bias.reshape(1, -1),
        norm_gain.reshape(1, -1),
        gate_bias,
        candidates,
        pre_inner,
        pre_outer,
        query_weight,
        history_kv,
        history_bias,
        expert_weight,
        gate_weight,
        tower_inner,
        tower_outer,
    )
    return score, jnp.transpose(rank, (1, 0, 2))


def solution(mesh):
    return jax.shard_map(
        on_device,
        mesh=mesh,
        in_specs=(
            P("groups", ("wide", "narrow"), None),
            P(),
            P(),
            P(),
            P("groups", None),
            P("groups", None),
            P("groups"),
            P(("groups", "wide"), None, None, "narrow"),
            P(("groups", "wide"), "narrow", None),
            P(("groups", "wide")),
            P(),
            P(),
            P("narrow", None, None),
            P(),
            P(),
            P("narrow", None, None),
            P("narrow", None),
        ),
        out_specs=(P("groups", ("wide", "narrow")), P(None, "groups", ("wide", "narrow"))),
        check_vma=False,
    )
```

```python
import functools

import jax
import jax.numpy as jnp
from jax import lax
from jax.experimental import pallas as pl
from jax.experimental.pallas import tpu as pltpu
from jax.sharding import PartitionSpec as P

F32 = jnp.float32
BF16 = jnp.bfloat16
MESH = pl.DeviceIdType.MESH


def quotient(x, n):
    if n & (n - 1) == 0:
        return lax.shift_right_logical(x, jnp.full_like(x, n.bit_length() - 1))
    return lax.div(x, jnp.full_like(x, n))


def iota(shape, dim):
    return lax.broadcasted_iota(jnp.int32, shape, dim)


def loop(count, body):
    if count <= 16:
        for i in range(count):
            body(i)
    else:
        lax.fori_loop(0, count, lambda i, _: (body(i), 0)[1], 0)


def dot(a, b, dims=((1,), (0,))):
    return lax.dot_general(a, b, (dims, ((), ())), preferred_element_type=F32)


def cascade(
    wide,
    narrow,
    block,
    slot_request,
    length,
    kept,
    user,
    pre_bias,
    norm_gain,
    gate_bias,
    cand_hbm,
    inner_hbm,
    outer_hbm,
    query_hbm,
    kv_hbm,
    bias_hbm,
    expert_hbm,
    gate_hbm,
    tower_hbm,
    last_hbm,
    score_out,
    rank_out,
    cand,
    inner,
    outer,
    query,
    kv,
    bias,
    expert,
    gate,
    tower,
    last,
    outgoing,
    arrived,
    compaction,
    expert_out,
    mixed,
    going,
    returned,
    local_sem,
    row_send,
    row_recv,
    swap_send,
    swap_recv,
    back_send,
    back_recv,
):
    w = lax.axis_index("wide")
    n = lax.axis_index("narrow")
    shards = wide * narrow
    me = w * narrow + n
    requests, shard_len, _ = cand.shape
    kept_count = kept.shape[1]
    rows = kept_count // narrow
    tasks = gate_bias.shape[0]
    experts = gate_bias.shape[1]
    heads_here = bias.shape[1]

    barrier = pltpu.get_barrier_semaphore()

    def greet(k):
        d = lax.rem(me + k + 1, shards)
        pl.semaphore_signal(
            barrier,
            inc=1,
            device_id={"wide": d // narrow, "narrow": lax.rem(d, narrow)},
            device_id_type=MESH,
        )

    loop(shards - 1, greet)

    plain = [
        pltpu.make_async_copy(src, dst, local_sem.at[k])
        for k, (src, dst) in enumerate(
            (
                (cand_hbm, cand),
                (inner_hbm, inner),
                (outer_hbm, outer),
                (query_hbm, query),
                (gate_hbm, gate),
            )
        )
    ]
    shared = ((kv_hbm.at[0], kv), (bias_hbm.at[0], bias), (expert_hbm, expert), (tower_hbm, tower), (last_hbm, last))
    own = [
        pltpu.make_async_copy(src, dst.at[n], local_sem.at[len(plain) + k])
        for k, (src, dst) in enumerate(shared)
    ]
    for copy in plain + own:
        copy.start()

    base = me * shard_len
    local = base + iota((shard_len, 1), 0)

    def pack(req, emb):
        row = kept[pl.ds(req, 1), :]
        below = jnp.sum((row < local).astype(F32), axis=1, keepdims=True).astype(jnp.int32)
        here = jnp.sum((row == local).astype(F32), axis=1, keepdims=True) > 0.5
        start = below[0:1]
        level = quotient(below, narrow)
        core = below - level * narrow
        place = level - quotient(start + (narrow - 1) - core, narrow)
        place = jnp.where(here, core * block + place, -1)
        packing = (place == iota((1, narrow * block), 1)).astype(F32).astype(BF16)
        return dot(packing, emb, ((0,), (0,))).astype(BF16)

    def score(req, emb):
        every = dot(user[...], emb, ((1,), (1,)))
        score_out[...] += jnp.where(iota((requests, 1), 0) == req, every, 0.0)

    score_out[...] = jnp.zeros_like(score_out)
    for copy in plain[:3]:
        copy.wait()

    def row_copy(i, g, p):
        return pltpu.make_async_remote_copy(
            src_ref=outgoing.at[i, p],
            dst_ref=arrived.at[me],
            send_sem=row_send.at[i, p],
            recv_sem=row_recv.at[me],
            device_id={"wide": g, "narrow": p},
            device_id_type=MESH,
        )

    def embed(x):
        hidden = jnp.maximum(dot(x, inner[...]) + pre_bias[...], 0.0).astype(BF16)
        return dot(hidden, outer[...]).astype(BF16)

    def serve(i, g, req, emb):
        packed = pack(req, emb)
        for p in range(narrow):
            outgoing[i, p] = packed[p * block : (p + 1) * block]

    def send(i, g):
        for p in range(narrow):
            row_copy(i, g, p).start()

    def swaps(k):
        other = lax.rem(n + k, narrow)
        return [
            pltpu.make_async_remote_copy(
                src_ref=src,
                dst_ref=dst.at[n],
                send_sem=swap_send.at[k, a],
                recv_sem=swap_recv.at[k, a],
                device_id={"narrow": other},
                device_id_type=MESH,
            )
            for a, (src, dst) in enumerate(shared)
        ]

    pair = 2 if shard_len % 16 == 0 and wide % 2 == 0 and wide <= 16 else 1
    if pair == 2:
        order = sorted(range(wide), key=lambda d: (abs(2 * d - wide), d))
        order = [d for d in order if d] + [0]
        for first in range(0, wide, 2):
            slots = [lax.rem(w + order[first + a], wide) for a in range(2)]
            reqs = [slot_request[g] for g in slots]
            both = embed(jnp.concatenate([cand[r] for r in reqs], axis=0))
            for a in range(2):
                emb = both[a * shard_len : (a + 1) * shard_len]
                serve(first + a, slots[a], reqs[a], emb)
                score(reqs[a], emb)
            if first == 0:
                pl.semaphore_wait(barrier, shards - 1)
            for a in range(2):
                if order[first + a]:
                    send(first + a, slots[a])
            if first == 2 or wide == 2:
                for k in range(1, narrow):
                    for copy in swaps(k):
                        copy.start()
    else:
        pl.semaphore_wait(barrier, shards - 1)
        for k in range(1, narrow):
            for copy in swaps(k):
                copy.start()

        def one(i):
            g = lax.rem(w + i + 1, wide)
            req = slot_request[g]
            emb = embed(cand[req])
            serve(i, g, req, emb)
            score(req, emb)

        def one_sent(i):
            one(i)
            send(i, lax.rem(w + i + 1, wide))

        loop(wide - 1, one_sent)
        one(wide - 1)
    for k in range(1, narrow):
        row_copy(wide - 1, w, lax.rem(n + k, narrow)).start()
    arrived[me] = outgoing[wide - 1, n]

    request = slot_request[w]
    row = kept[pl.ds(request, 1), :].astype(F32)
    column = jnp.transpose(jnp.broadcast_to(row, (128, kept_count)))[:, 0:1]
    rank = jnp.sum((column < row).astype(F32), axis=0, keepdims=True)
    line = iota((rows, 1), 0)
    wanted = (line * narrow + n).astype(F32)
    chosen = jnp.sum(jnp.where(rank == wanted, row, 0.0), axis=1, keepdims=True)
    chosen = chosen.astype(jnp.int32)
    shard = quotient(chosen, shard_len)
    start = jnp.sum(
        (row < (shard * shard_len).astype(F32)).astype(F32), axis=1, keepdims=True
    ).astype(jnp.int32)
    spot = shard * block + line - quotient(start + (narrow - 1) - n, narrow)
    compaction[...] = (spot == iota((1, shards * block), 1)).astype(F32).astype(BF16)

    for copy in plain[3:] + own:
        copy.wait()
    for k in range(1, narrow):
        for copy in swaps(k):
            copy.wait_recv()

    def rows_in(k):
        d = lax.rem(me + k + 1, shards)
        pltpu.make_async_remote_copy(
            src_ref=outgoing.at[0, 0],
            dst_ref=arrived.at[d],
            send_sem=row_send.at[0, 0],
            recv_sem=row_recv.at[d],
            device_id={"wide": d // narrow, "narrow": lax.rem(d, narrow)},
            device_id_type=MESH,
        ).wait_recv()

    loop(shards - 1, rows_in)
    width = arrived.shape[2]
    embedded = dot(compaction[...], arrived[...].reshape(shards * block, width)).astype(BF16)
    heads = heads_here * narrow
    size = query.shape[1] // heads
    queries = dot(embedded, query[...]).astype(BF16).astype(F32) * float(size) ** (-0.5)
    span = kv.shape[2]
    seen = iota((1, span), 1) < length[0]
    side = 128 // size if 128 % size == 0 and heads_here % (128 // size) == 0 else 1
    strip = side * size
    lane = iota((1, strip), 1)
    pieces = []
    for first in range(0, heads, side):
        c, h = first // heads_here, first % heads_here
        keys = kv[c, 0, :, h * size : h * size + strip]
        values = kv[c, 1, :, h * size : h * size + strip]
        q = queries[:, first * size : first * size + strip]
        out = None
        for a in range(side):
            mine = (lane >= a * size) & (lane < (a + 1) * size)
            s = dot(jnp.where(mine, q, 0.0).astype(BF16), keys, ((1,), (1,)))
            s = s + jnp.where(seen, bias[c, h + a : h + a + 1, :], -jnp.inf)
            top = jnp.max(s, axis=1, keepdims=True)
            powers = jnp.exp(s - top)
            total = jnp.sum(powers, axis=1, keepdims=True)
            part = dot(powers.astype(BF16), values) / total
            out = part if out is None else jnp.where(mine, part, out)
        pieces.append(out.astype(BF16))
    attended = jnp.concatenate(pieces, axis=1)
    u = embedded.astype(F32) + attended.astype(F32)
    normed = (
        u * lax.rsqrt(jnp.mean(u * u, axis=1, keepdims=True) + 1e-06) * norm_gain[...]
    ).astype(BF16)

    logits = dot(gate[...], normed, ((1,), (1,)))
    diagonal = iota((experts, experts), 0) == iota((experts, experts), 1)
    probs = []
    for t in range(tasks):
        offset = jnp.sum(
            jnp.where(diagonal, gate_bias[t : t + 1, :], 0.0), axis=1, keepdims=True
        )
        x = logits[t * experts : (t + 1) * experts] + offset
        x = jnp.exp(x - jnp.max(x, axis=0, keepdims=True))
        probs.append(x / jnp.sum(x, axis=0, keepdims=True))
    fill = -(tasks * experts) % 128
    if fill:
        probs.append(jnp.zeros((fill, rows), F32))
    probs = jnp.transpose(jnp.concatenate(probs, axis=0).astype(BF16).astype(F32))

    experts_here = expert.shape[1]
    for e in range(experts):
        out = dot(normed, expert[e // experts_here, e % experts_here])
        expert_out[e] = jnp.maximum(out, 0.0).astype(BF16).astype(F32)
    step = 64 if rows % 64 == 0 else rows
    for t in range(tasks):
        for r in range(0, rows, step):
            acc = None
            for e in range(experts):
                k = t * experts + e
                term = probs[r : r + step, k : k + 1] * expert_out[e, r : r + step]
                acc = term if acc is None else acc + term
            mixed[t, r : r + step] = acc.astype(BF16)
    tasks_here = tower.shape[1]
    final = jnp.zeros((tasks, rows), F32)
    for t in range(tasks):
        c, h = t // tasks_here, t % tasks_here
        act = jnp.maximum(dot(mixed[t], tower[c, h]), 0.0).astype(BF16)
        weights = last[c, h : h + 1, :].astype(F32)
        weights = jnp.where(iota((tasks, 1), 0) == t, weights, 0.0).astype(BF16)
        final = final + dot(weights, act, ((1,), (1,)))

    high = final.astype(BF16)
    rest = final - high.astype(F32)
    middle = rest.astype(BF16)
    low = (rest - middle.astype(F32)).astype(BF16)
    lanes = going.shape[2]

    def back_copy(d):
        return pltpu.make_async_remote_copy(
            src_ref=going.at[d],
            dst_ref=returned.at[me],
            send_sem=back_send.at[d],
            recv_sem=back_recv.at[me],
            device_id={"wide": d // narrow, "narrow": lax.rem(d, narrow)},
            device_id_type=MESH,
        )

    def scatter(k):
        d = lax.rem(me + k + 1, shards)
        spread = (chosen == d * shard_len + iota((1, lanes), 1)).astype(F32).astype(BF16)
        going[d] = dot(high, spread) + dot(middle, spread) + dot(low, spread)

    def scatter_send(k):
        scatter(k)
        back_copy(lax.rem(me + k + 1, shards)).start()

    loop(shards - 1, scatter_send)
    scatter(shards - 1)
    returned[me] = going[me]

    def back_in(k):
        d = lax.rem(me + k + 1, shards)
        pltpu.make_async_remote_copy(
            src_ref=going.at[0],
            dst_ref=returned.at[d],
            send_sem=back_send.at[0],
            recv_sem=back_recv.at[d],
            device_id={"wide": d // narrow, "narrow": lax.rem(d, narrow)},
            device_id_type=MESH,
        ).wait_recv()

    loop(shards - 1, back_in)

    def deliver(r):
        if requests <= 16:
            slot = 0
            for g in range(requests):
                slot = jnp.where(slot_request[g] == r, g, slot)
        else:
            slot = lax.fori_loop(
                0, requests, lambda g, a: jnp.where(slot_request[g] == r, g, a), 0
            )
        total = returned[slot * narrow]
        for p in range(1, narrow):
            total = total + returned[slot * narrow + p]
        rank_out[:, r, :] = total[:, :shard_len]

    loop(requests, deliver)

    def rows_out(i):
        for p in range(narrow):
            row_copy(i, w, p).wait_send()

    loop(wide - 1, rows_out)
    for k in range(1, narrow):
        row_copy(wide - 1, w, lax.rem(n + k, narrow)).wait_send()
        for copy in swaps(k):
            copy.wait_send()
    loop(shards - 1, lambda k: back_copy(lax.rem(me + k + 1, shards)).wait_send())


def on_device(
    candidates,
    pre_inner,
    pre_bias,
    pre_outer,
    user_vector,
    kept_index,
    slot_request,
    history_kv,
    history_bias,
    history_length,
    query_weight,
    norm_gain,
    expert_weight,
    gate_weight,
    gate_bias,
    tower_inner,
    tower_outer,
):
    wide = lax.axis_size("wide")
    narrow = lax.axis_size("narrow")
    shards = wide * narrow
    requests, shard_len, features = candidates.shape
    kept_count = kept_index.shape[1]
    assert history_kv.shape[0] == 1 and requests == wide and kept_count % narrow == 0
    capacity = 2 * kept_count // shards
    block = -(-capacity // narrow)
    block = -(-block // 16) * 16
    rows = kept_count // narrow
    width = pre_outer.shape[1]
    tasks, experts = gate_bias.shape
    hidden = expert_weight.shape[2]
    lanes = max(shard_len, 128)
    smem = pl.BlockSpec(memory_space=pltpu.SMEM)
    vmem = pl.BlockSpec(memory_space=pltpu.VMEM)
    hbm = pl.BlockSpec(memory_space=pl.ANY)

    def whole(x):
        return pltpu.VMEM(x.shape, x.dtype)

    def both(x):
        return pltpu.VMEM((narrow, *x.shape), x.dtype)

    score, rank = pl.pallas_call(
        functools.partial(cascade, wide, narrow, block),
        out_shape=(
            jax.ShapeDtypeStruct((requests, shard_len), F32),
            jax.ShapeDtypeStruct((tasks, requests, shard_len), F32),
        ),
        in_specs=[smem] * 2 + [vmem] * 5 + [hbm] * 10,
        out_specs=(vmem, vmem),
        scratch_shapes=[
            whole(candidates),
            whole(pre_inner),
            whole(pre_outer),
            whole(query_weight),
            pltpu.VMEM((narrow, *history_kv.shape[1:]), BF16),
            pltpu.VMEM((narrow, *history_bias.shape[1:]), F32),
            both(expert_weight),
            pltpu.VMEM(gate_weight.shape[::-1], BF16),
            both(tower_inner),
            both(tower_outer),
            pltpu.VMEM((wide, narrow, block, width), BF16),
            pltpu.VMEM((shards, block, width), BF16),
            pltpu.VMEM((rows, shards * block), BF16),
            pltpu.VMEM((experts, rows, hidden), F32),
            pltpu.VMEM((tasks, rows, hidden), BF16),
            pltpu.VMEM((shards, tasks, lanes), F32),
            pltpu.VMEM((shards, tasks, lanes), F32),
            pltpu.SemaphoreType.DMA((10,)),
            pltpu.SemaphoreType.DMA((wide, narrow)),
            pltpu.SemaphoreType.DMA((shards,)),
            pltpu.SemaphoreType.DMA((narrow, 5)),
            pltpu.SemaphoreType.DMA((narrow, 5)),
            pltpu.SemaphoreType.DMA((shards,)),
            pltpu.SemaphoreType.DMA((shards,)),
        ],
        compiler_params=pltpu.CompilerParams(
            collective_id=0, has_side_effects=True, vmem_limit_bytes=56 * 1024 * 1024
        ),
    )(
        slot_request,
        history_length,
        kept_index,
        user_vector,
        pre_bias.reshape(1, -1),
        norm_gain.reshape(1, -1),
        gate_bias,
        candidates,
        pre_inner,
        pre_outer,
        query_weight,
        history_kv,
        history_bias,
        expert_weight,
        gate_weight.T,
        tower_inner,
        tower_outer,
    )
    return score, rank


def solution(mesh):
    return jax.shard_map(
        on_device,
        mesh=mesh,
        in_specs=(
            P("groups", ("wide", "narrow"), None),
            P(),
            P(),
            P(),
            P("groups", None),
            P("groups", None),
            P("groups"),
            P(("groups", "wide"), None, None, "narrow"),
            P(("groups", "wide"), "narrow", None),
            P(("groups", "wide")),
            P(),
            P(),
            P("narrow", None, None),
            P(),
            P(),
            P("narrow", None, None),
            P("narrow", None),
        ),
        out_specs=(P("groups", ("wide", "narrow")), P(None, "groups", ("wide", "narrow"))),
        check_vma=False,
    )
```
